32 devices in a mesh: parts: 2 (over x), seq: 16 (over z, y, core).
Axes of the slice: x: 2, y: 2, z: 4, core: 2. Of those that a mesh axis runs over, the one named last changes fastest.
Arguments:
- tokens: bfloat16 [131072, 512], P(('parts', 'seq')), parts along dimension 0, may hold values from -6 to 6
- w_value: bfloat16 [512, 512], replicated, may hold values from -0.25 to 0.25
- w_gate: bfloat16 [512, 512], replicated, may hold values from -0.25 to 0.25
- first_block: bfloat16 [256, 256], replicated, may hold values from -0.375 to 0.375
- second_block: bfloat16 [256, 256], replicated, may hold values from -0.375 to 0.375
- third_block: bfloat16 [256, 256], replicated, may hold values from -0.375 to 0.375
- fourth_block: bfloat16 [256, 256], replicated, may hold values from -0.375 to 0.375
- kernel: bfloat16 [512, 256, 256], P('seq'), may hold values from -6 to 6
- skip_gain: float32 [512], replicated, may hold values from 0.25 to 2
- cotangent: bfloat16 [131072, 512], P(('parts', 'seq')), parts along dimension 0, may hold values from -6 to 6
Outputs:
- grad_tokens: bfloat16 [131072, 512], P(('parts', 'seq')), parts along dimension 0
- grad_kernel: bfloat16 [1024, 256, 256], P(('parts', 'seq')), parts along dimension 0
- grad_weights: float32 [4, 512, 512], P('parts'), parts along dimension 0
- grad_skip: float32 [1024], P('parts'), parts along dimension 0
The draws below stay inside these ranges and needn't reach their ends.
There are 2 independent parts, one for each index of `parts`. The reference program is written for one: setup_inputs(seed, part) draws one part's arguments, and reference() takes and returns one part's arrays. A program takes and returns all parts, laid end to end along the dimension named above; an argument that names none is the same for every part. Nothing has to cross between parts.
All inputs are finite; a program needn't handle non-finite values.
Results may differ from the reference program's by a relative error of at most 0.025.
Values may be sent and summed in bfloat16 or wider, within the bound.
A program may use at most 128 MiB of HBM per device.

```python
import math
import jax
import jax.numpy as jnp
from jax import lax

D = 512
N1 = 256
N2 = 256
LEN = 65536


def level_of(key, extent, split, least, top_value):
    gain = 1.0
    for position, blocks in split:
        draws = jax.random.uniform(jax.random.fold_in(jax.random.fold_in(key, 6), position), (blocks,), jnp.float32, least / len(split), top_value / len(split))
        gain = gain * jnp.repeat(jnp.exp(draws), extent[position] // blocks).reshape((-1,) + (1,) * (len(extent) - 1 - position))
    return gain


def scatter_about(own_key, extent, spread, reach, split=(), dtype=jnp.bfloat16):
    array = jax.random.normal(own_key, extent, jnp.float32) * spread
    if len(split) > 0:
        array = level_of(own_key, extent, split, -0.22, 0.18) * array
    return jnp.clip(array, min=-reach, max=reach).astype(dtype)


def setup_inputs(seed: int = 0, part: int = 0) -> dict:
    key_list = jax.random.split(jax.random.key(seed), 11)
    own_keys = jax.random.split(jax.random.fold_in(key_list[10], part), 11)
    tokens = scatter_about(own_keys[0], (LEN, D), 1.0, 6.0, ((0, 16),))
    w_value = scatter_about(key_list[1], (D, D), D ** -0.5, 0.25)
    w_gate = scatter_about(key_list[2], (D, D), D ** -0.5, 0.25)
    first_block = scatter_about(key_list[3], (N2, N2), N2 ** -0.5, 0.375)
    second_block = scatter_about(key_list[4], (N1, N1), N1 ** -0.5, 0.375)
    third_block = scatter_about(key_list[5], (N1, N1), N1 ** -0.5, 0.375)
    fourth_block = scatter_about(key_list[6], (N2, N2), N2 ** -0.5, 0.375)
    kernel = scatter_about(key_list[7], (D, N1, N2), 1.0, 6.0, ((0, 16),))
    skip_gain = jnp.clip(jnp.exp(jax.random.uniform(key_list[8], (D,), jnp.float32, math.log(0.25), math.log(2.0))), 0.25, 2.0)
    cotangent = scatter_about(own_keys[9], (LEN, D), 1.0, 6.0, ((0, 16),))
    return {"tokens": tokens, "w_value": w_value, "w_gate": w_gate, "first_block": first_block, "second_block": second_block, "third_block": third_block, "fourth_block": fourth_block, "kernel": kernel, "skip_gain": skip_gain, "cotangent": cotangent}


def reference(tokens, w_value, w_gate, first_block, second_block, third_block, fourth_block, kernel, skip_gain, cotangent):
    f32 = jnp.float32
    bf16 = jnp.bfloat16
    length = N1 * N2
    value = jnp.dot(tokens, w_value, preferred_element_type=f32).astype(bf16)
    gate = jnp.dot(tokens, w_gate, preferred_element_type=f32).astype(bf16)
    cube = value.reshape(N1, N2, D).astype(f32)
    section_one = jnp.einsum('abc,pb->apc', cube, first_block.astype(f32)).astype(bf16)
    spectrum = jnp.einsum('apc,qa->qpc', section_one.astype(f32), second_block.astype(f32))
    kernel_t = jnp.transpose(kernel.astype(f32), (1, 2, 0))
    filtered = (spectrum * kernel_t).astype(bf16)
    section_three = jnp.einsum('qpc,rq->rpc', filtered.astype(f32), third_block.astype(f32)).astype(bf16)
    conv = jnp.einsum('rpc,sp->rsc', section_three.astype(f32), fourth_block.astype(f32)).reshape(length, D)
    mixed = conv + skip_gain * value.astype(f32)
    upstream = cotangent.astype(f32)
    d_mix = (upstream * gate.astype(f32)).astype(bf16)
    d_gate = (upstream * mixed).astype(bf16)
    d_three = jnp.einsum('rsc,sp->rpc', d_mix.reshape(N1, N2, D).astype(f32), fourth_block.astype(f32)).astype(bf16)
    d_freq = jnp.einsum('rpc,rq->qpc', d_three.astype(f32), third_block.astype(f32))
    grad_kernel = jnp.transpose((d_freq * spectrum).astype(bf16), (2, 0, 1))
    d_spec = (d_freq * kernel_t).astype(bf16)
    d_one = jnp.einsum('qpc,qa->apc', d_spec.astype(f32), second_block.astype(f32)).astype(bf16)
    d_cube = jnp.einsum('apc,pb->abc', d_one.astype(f32), first_block.astype(f32)).reshape(length, D)
    d_value = (d_cube + skip_gain * d_mix.astype(f32)).astype(bf16)
    grad_tokens = (jnp.dot(d_value, w_value.T, preferred_element_type=f32) + jnp.dot(d_gate, w_gate.T, preferred_element_type=f32)).astype(bf16)
    factor = 1.0 / jnp.sqrt(jnp.asarray(length, f32))
    grad_value_w = jnp.dot(tokens.T, d_value, preferred_element_type=f32) * factor
    grad_gate_w = jnp.dot(tokens.T, d_gate, preferred_element_type=f32) * factor
    grad_skip = lax.optimization_barrier(jnp.sum(d_mix.astype(f32) * value.astype(f32), axis=0)) * factor
    return (grad_tokens, grad_kernel, jnp.stack([grad_value_w, grad_gate_w]), grad_skip)
```

```python
import functools

import jax
import jax.numpy as jnp
from jax import lax
from jax.experimental import pallas as pl
from jax.experimental.pallas import tpu as pltpu
from jax.sharding import PartitionSpec as P

MESH = pl.DeviceIdType.MESH
f32 = jnp.float32
bf16 = jnp.bfloat16


def reduce_kernel(n, x_ref, s_ref, out_ref, skip_ref, pair, mine, slots, skips, rs_send, rs_recv, ag_send, ag_recv, sk_send, sk_recv, ps_send, ps_recv):
    me = lax.axis_index("seq")
    core = lax.rem(me, 2)
    chip = lax.div(me, 2)
    chips = n // 2
    partner = me + 1 - 2 * core
    rows = x_ref.shape[0]
    half = rows // 2
    part = half // chips

    barrier = pltpu.get_barrier_semaphore()

    def greet(k, carry):
        peer = lax.rem(me + k, n)
        pl.semaphore_signal(barrier, inc=1, device_id={"seq": peer}, device_id_type=MESH)
        return carry

    lax.fori_loop(1, n, greet, 0)
    pl.semaphore_wait(barrier, n - 1)

    other_half = pl.ds(pl.multiple_of((1 - core) * half, half), half)
    first = pltpu.make_async_remote_copy(
        src_ref=x_ref.at[other_half], dst_ref=pair, send_sem=ps_send, recv_sem=ps_recv,
        device_id={"seq": partner}, device_id_type=MESH)
    first.start()

    def skip_copy(k):
        peer = lax.rem(me + k, n)
        return pltpu.make_async_remote_copy(
            src_ref=s_ref, dst_ref=skips.at[k], send_sem=sk_send.at[k], recv_sem=sk_recv.at[k],
            device_id={"seq": peer}, device_id_type=MESH)

    lax.fori_loop(1, n, lambda k, c: (skip_copy(k).start(), c)[1], 0)
    first.wait()
    my_half = pl.ds(pl.multiple_of(core * half, half), half)
    mine[...] = (x_ref[my_half, :].astype(f32) + pair[...].astype(f32)).astype(bf16)

    def rs_copy(k):
        peer_chip = lax.rem(chip + k, chips)
        src = pl.ds(pl.multiple_of(peer_chip * part, part), part)
        return pltpu.make_async_remote_copy(
            src_ref=mine.at[src], dst_ref=slots.at[k], send_sem=rs_send.at[k], recv_sem=rs_recv.at[k],
            device_id={"seq": 2 * peer_chip + core}, device_id_type=MESH)

    lax.fori_loop(1, chips, lambda k, c: (rs_copy(k).start(), c)[1], 0)
    own = pl.ds(pl.multiple_of(chip * part, part), part)

    def rs_add(k, total):
        rs_copy(k).wait_recv()
        return total + slots[k].astype(f32)

    total = lax.fori_loop(1, chips, rs_add, mine[own, :].astype(f32))
    lax.fori_loop(1, chips, lambda k, c: (rs_copy(k).wait_send(), c)[1], 0)
    place = pl.ds(pl.multiple_of(core * half + chip * part, part), part)
    out_ref[place, :] = total.astype(bf16)

    def ag_copy(k):
        peer = lax.rem(me + k, n)
        return pltpu.make_async_remote_copy(
            src_ref=out_ref.at[place], dst_ref=out_ref.at[place], send_sem=ag_send.at[k], recv_sem=ag_recv.at[k],
            device_id={"seq": peer}, device_id_type=MESH)

    lax.fori_loop(1, n, lambda k, c: (ag_copy(k).start(), c)[1], 0)

    skips[0] = s_ref[...]
    lax.fori_loop(1, n, lambda k, c: (skip_copy(k).wait(), c)[1], 0)

    def skip_add(d, total):
        return total + skips[lax.rem(me - d + n, n)]

    skip_ref[...] = lax.fori_loop(0, n, skip_add, jnp.zeros(s_ref.shape, f32))

    def ag_wait(k, carry):
        ag_copy(k).wait_send()
        ag_copy(k).wait_recv()
        return carry

    lax.fori_loop(1, n, ag_wait, 0)


def all_sum(x, s, n):
    rows, cols = x.shape
    half = rows // 2
    chips = n // 2
    dma = pltpu.SemaphoreType.DMA
    return pl.pallas_call(
        functools.partial(reduce_kernel, n),
        out_shape=(jax.ShapeDtypeStruct(x.shape, bf16), jax.ShapeDtypeStruct(s.shape, f32)),
        in_specs=[pl.BlockSpec(memory_space=pltpu.VMEM)] * 2,
        out_specs=(pl.BlockSpec(memory_space=pltpu.VMEM),) * 2,
        scratch_shapes=[
            pltpu.VMEM((half, cols), bf16),
            pltpu.VMEM((half, cols), bf16),
            pltpu.VMEM((chips, half // chips, cols), bf16),
            pltpu.VMEM((n,) + s.shape, f32),
            dma((chips,)), dma((chips,)), dma((n,)), dma((n,)), dma((n,)), dma((n,)), dma, dma,
        ],
        compiler_params=pltpu.CompilerParams(collective_id=0, has_side_effects=True),
        name="all_sum",
    )(x, s)


def on_device(tokens, w_value, w_gate, first_block, second_block, third_block, fourth_block, kernel, skip_gain, cotangent):
    n = lax.axis_size("seq")
    n1 = second_block.shape[0]
    n2 = first_block.shape[0]
    local_rows, d = tokens.shape
    rows_here = n1 // n
    value = jnp.dot(tokens, w_value, preferred_element_type=f32).astype(bf16)
    cube = value.reshape(rows_here, n2, d)
    section_one = jnp.einsum("abc,pb->cap", cube, first_block, preferred_element_type=f32).astype(bf16)
    one_here = lax.all_to_all(section_one, "seq", split_axis=0, concat_axis=1, tiled=True)

    gate = jnp.dot(tokens, w_gate, preferred_element_type=f32).astype(bf16)
    upstream = cotangent.astype(f32)
    d_mix = (upstream * gate.astype(f32)).astype(bf16)
    d_mix_cube = d_mix.reshape(rows_here, n2, d)
    d_three = jnp.einsum("rsc,sp->crp", d_mix_cube, fourth_block, preferred_element_type=f32).astype(bf16)
    skip_term = jnp.sum(d_mix.astype(f32) * value.astype(f32), axis=0)
    one_here, d_three, skip_term = lax.optimization_barrier((one_here, d_three, skip_term))
    three_here = lax.all_to_all(d_three, "seq", split_axis=0, concat_axis=1, tiled=True)

    spectrum = jnp.einsum("cap,qa->cqp", one_here, second_block, preferred_element_type=f32)
    filtered = (spectrum * kernel.astype(f32)).astype(bf16)
    section_three = jnp.einsum("cqp,rq->crp", filtered, third_block, preferred_element_type=f32).astype(bf16)
    split_three = section_three.reshape(section_three.shape[0], n, rows_here, n2)
    three_here, split_three, spectrum = lax.optimization_barrier((three_here, split_three, spectrum))
    back_three = lax.all_to_all(split_three, "seq", split_axis=1, concat_axis=0, tiled=True)[:, 0]

    d_freq = jnp.einsum("crp,rq->cqp", three_here, third_block, preferred_element_type=f32)
    grad_kernel = (d_freq * spectrum).astype(bf16)
    d_spec = (d_freq * kernel.astype(f32)).astype(bf16)
    d_one = jnp.einsum("cqp,qa->cap", d_spec, second_block, preferred_element_type=f32).astype(bf16)
    split_one = d_one.reshape(d_one.shape[0], n, rows_here, n2)
    back_three, split_one, grad_kernel = lax.optimization_barrier((back_three, split_one, grad_kernel))
    back_one = lax.all_to_all(split_one, "seq", split_axis=1, concat_axis=0, tiled=True)[:, 0]

    conv = jnp.einsum("crp,sp->rsc", back_three, fourth_block, preferred_element_type=f32)
    mixed = conv.reshape(local_rows, d) + skip_gain * value.astype(f32)
    d_gate = (upstream * mixed).astype(bf16)
    factor = 1.0 / jnp.sqrt(jnp.asarray(n1 * n2, f32))
    gate_term = (jnp.dot(tokens.T, d_gate, preferred_element_type=f32) * factor).astype(bf16)
    gate_grad = jnp.dot(d_gate, w_gate.T, preferred_element_type=f32)
    back_one, gate_term, gate_grad = lax.optimization_barrier((back_one, gate_term, gate_grad))

    d_cube = jnp.einsum("cap,pb->abc", back_one, first_block, preferred_element_type=f32)
    d_value = (d_cube.reshape(local_rows, d) + skip_gain * d_mix.astype(f32)).astype(bf16)
    grad_tokens = (jnp.dot(d_value, w_value.T, preferred_element_type=f32) + gate_grad).astype(bf16)
    value_term = (jnp.dot(tokens.T, d_value, preferred_element_type=f32) * factor).astype(bf16)
    skip_rows = jnp.pad((skip_term * factor).reshape(-1, 128), ((0, 8 - d // 128), (0, 0)))
    sums, skip_sum = all_sum(jnp.concatenate([value_term, gate_term]), skip_rows, n)
    return (grad_tokens, grad_kernel, sums.astype(f32).reshape(2, d, d), skip_sum[: d // 128].reshape(d))


def solution(mesh):
    in_specs = (
        P(("parts", "seq"), None), P(), P(), P(), P(), P(), P(), P("seq", None, None), P(), P(("parts", "seq"), None),
    )
    out_specs = (
        P(("parts", "seq"), None), P(("parts", "seq"), None, None), P("parts", None, None), P("parts"),
    )
    return jax.shard_map(on_device, mesh=mesh, in_specs=in_specs, out_specs=out_specs, check_vma=False)
```

```python
import functools

import jax
import jax.numpy as jnp
from jax import lax
from jax.experimental import pallas as pl
from jax.experimental.pallas import tpu as pltpu
from jax.sharding import PartitionSpec as P

MESH = pl.DeviceIdType.MESH
f32 = jnp.float32
bf16 = jnp.bfloat16


def reduce_kernel(n, x_ref, s_ref, out_ref, skip_ref, pair, mine, slots, skips, rs_send, rs_recv, ag_send, ag_recv, fw_send, fw_recv, sk_send, sk_recv, ps_send, ps_recv):
    me = lax.axis_index("seq")
    core = lax.rem(me, 2)
    chip = lax.div(me, 2)
    chips = n // 2
    partner = me + 1 - 2 * core
    rows = x_ref.shape[0]
    half = rows // 2
    part = half // chips

    barrier = pltpu.get_barrier_semaphore()

    def greet(k, carry):
        peer = lax.rem(me + k, n)
        pl.semaphore_signal(barrier, inc=1, device_id={"seq": peer}, device_id_type=MESH)
        return carry

    lax.fori_loop(1, n, greet, 0)
    pl.semaphore_wait(barrier, n - 1)

    other_half = pl.ds(pl.multiple_of((1 - core) * half, half), half)
    first = pltpu.make_async_remote_copy(
        src_ref=x_ref.at[other_half], dst_ref=pair, send_sem=ps_send, recv_sem=ps_recv,
        device_id={"seq": partner}, device_id_type=MESH)
    first.start()

    def skip_copy(k):
        peer = lax.rem(me + k, n)
        return pltpu.make_async_remote_copy(
            src_ref=s_ref, dst_ref=skips.at[k], send_sem=sk_send.at[k], recv_sem=sk_recv.at[k],
            device_id={"seq": peer}, device_id_type=MESH)

    lax.fori_loop(1, n, lambda k, c: (skip_copy(k).start(), c)[1], 0)
    first.wait()
    my_half = pl.ds(pl.multiple_of(core * half, half), half)
    mine[...] = (x_ref[my_half, :].astype(f32) + pair[...].astype(f32)).astype(bf16)

    def rs_copy(k):
        peer_chip = lax.rem(chip + k, chips)
        src = pl.ds(pl.multiple_of(peer_chip * part, part), part)
        return pltpu.make_async_remote_copy(
            src_ref=mine.at[src], dst_ref=slots.at[k], send_sem=rs_send.at[k], recv_sem=rs_recv.at[k],
            device_id={"seq": 2 * peer_chip + core}, device_id_type=MESH)

    lax.fori_loop(1, chips, lambda k, c: (rs_copy(k).start(), c)[1], 0)
    own = pl.ds(pl.multiple_of(chip * part, part), part)

    def rs_add(k, total):
        rs_copy(k).wait_recv()
        return total + slots[k].astype(f32)

    total = lax.fori_loop(1, chips, rs_add, mine[own, :].astype(f32))
    lax.fori_loop(1, chips, lambda k, c: (rs_copy(k).wait_send(), c)[1], 0)
    place = pl.ds(pl.multiple_of(core * half + chip * part, part), part)
    out_ref[place, :] = total.astype(bf16)

    def rows_of(k):
        source = lax.rem(chip - k + chips, chips)
        return pl.ds(pl.multiple_of(core * half + source * part, part), part)

    def ag_copy(k):
        peer_chip = lax.rem(chip + k, chips)
        return pltpu.make_async_remote_copy(
            src_ref=out_ref.at[place], dst_ref=out_ref.at[place], send_sem=ag_send.at[k], recv_sem=ag_recv.at[k],
            device_id={"seq": 2 * peer_chip + core}, device_id_type=MESH)

    def pass_on(k):
        return pltpu.make_async_remote_copy(
            src_ref=out_ref.at[rows_of(k)], dst_ref=out_ref.at[rows_of(k)], send_sem=fw_send.at[k], recv_sem=fw_recv.at[k],
            device_id={"seq": partner}, device_id_type=MESH)

    lax.fori_loop(1, chips, lambda k, c: (ag_copy(k).start(), c)[1], 0)
    pass_on(0).start()

    skips[0] = s_ref[...]
    lax.fori_loop(1, n, lambda k, c: (skip_copy(k).wait(), c)[1], 0)

    def skip_add(d, total):
        return total + skips[lax.rem(me - d + n, n)]

    skip_ref[...] = lax.fori_loop(0, n, skip_add, jnp.zeros(s_ref.shape, f32))

    def arrived(k, carry):
        ag_copy(k).wait_recv()
        pass_on(k).start()
        return carry

    lax.fori_loop(1, chips, arrived, 0)
    lax.fori_loop(1, chips, lambda k, c: (ag_copy(k).wait_send(), c)[1], 0)
    lax.fori_loop(0, chips, lambda k, c: (pass_on(k).wait(), c)[1], 0)


def all_sum(x, s, n):
    rows, cols = x.shape
    half = rows // 2
    chips = n // 2
    dma = pltpu.SemaphoreType.DMA
    return pl.pallas_call(
        functools.partial(reduce_kernel, n),
        out_shape=(jax.ShapeDtypeStruct(x.shape, bf16), jax.ShapeDtypeStruct(s.shape, f32)),
        in_specs=[pl.BlockSpec(memory_space=pltpu.VMEM)] * 2,
        out_specs=(pl.BlockSpec(memory_space=pltpu.VMEM),) * 2,
        scratch_shapes=[
            pltpu.VMEM((half, cols), bf16),
            pltpu.VMEM((half, cols), bf16),
            pltpu.VMEM((chips, half // chips, cols), bf16),
            pltpu.VMEM((n,) + s.shape, f32),
            dma((chips,)), dma((chips,)), dma((chips,)), dma((chips,)), dma((chips,)), dma((chips,)), dma((n,)), dma((n,)), dma, dma,
        ],
        compiler_params=pltpu.CompilerParams(collective_id=0, has_side_effects=True),
        name="all_sum",
    )(x, s)


def exchange_kernel(n, one_ref, three_ref, kern_ref, b_ref, bt_ref, g_ref, gt_ref, back3_ref, back1_ref, gk_ref,
                    held1, held3, spec, s1, r1, s3, r3, sb3, rb3, sb1, rb1, own):
    me = lax.axis_index("seq")
    wide = kern_ref.shape[0]
    rows = one_ref.shape[1]
    barrier = pltpu.get_barrier_semaphore()

    def greet(k, carry):
        pl.semaphore_signal(barrier, inc=1, device_id={"seq": lax.rem(me + k, n)}, device_id_type=MESH)
        return carry

    lax.fori_loop(1, n, greet, 0)
    pl.semaphore_wait(barrier, n - 1)

    def channels_of(d):
        return pl.ds(pl.multiple_of(d * wide, wide), wide)

    def rows_of(d):
        return pl.ds(pl.multiple_of(d * rows, rows), rows)

    def out_copy(src, dst, send, recv, k):
        peer = lax.rem(me + k, n)
        return pltpu.make_async_remote_copy(
            src_ref=src.at[channels_of(peer)], dst_ref=dst.at[:, rows_of(me), :], send_sem=send.at[k], recv_sem=recv.at[k],
            device_id={"seq": peer}, device_id_type=MESH)

    def back_copy(src, dst, send, recv, k):
        peer = lax.rem(me + k, n)
        return pltpu.make_async_remote_copy(
            src_ref=src.at[:, rows_of(peer), :], dst_ref=dst.at[channels_of(me)], send_sem=send.at[k], recv_sem=recv.at[k],
            device_id={"seq": peer}, device_id_type=MESH)

    def start_all(copy, *refs):
        lax.fori_loop(1, n, lambda k, c: (copy(*refs, k).start(), c)[1], 0)

    def wait_all(copy, *refs):
        lax.fori_loop(1, n, lambda k, c: (copy(*refs, k).wait(), c)[1], 0)

    first = (out_copy, one_ref, held1, s1, r1)
    second = (out_copy, three_ref, held3, s3, r3)
    third = (back_copy, held1, back3_ref, sb3, rb3)
    fourth = (back_copy, held3, back1_ref, sb1, rb1)
    start_all(*first)
    own1 = pltpu.make_async_copy(one_ref.at[channels_of(me)], held1.at[:, rows_of(me), :], own.at[0])
    own1.start()
    own3 = pltpu.make_async_copy(three_ref.at[channels_of(me)], held3.at[:, rows_of(me), :], own.at[1])
    own3.start()
    start_all(*second)

    own1.wait()
    wait_all(*first)

    def forward(c, carry):
        spectrum = jnp.dot(b_ref[...], held1[c], preferred_element_type=f32)
        spec[c] = spectrum
        filtered = (spectrum * kern_ref[c].astype(f32)).astype(bf16)
        held1[c] = jnp.dot(g_ref[...], filtered, preferred_element_type=f32).astype(bf16)
        return carry

    lax.fori_loop(0, wide, forward, 0)
    start_all(*third)
    keep3 = pltpu.make_async_copy(held1.at[:, rows_of(me), :], back3_ref.at[channels_of(me)], own.at[2])
    keep3.start()
    own3.wait()
    wait_all(*second)

    def backward(c, carry):
        d_freq = jnp.dot(gt_ref[...], held3[c], preferred_element_type=f32)
        gk_ref[c] = (d_freq * spec[c]).astype(bf16)
        d_spec = (d_freq * kern_ref[c].astype(f32)).astype(bf16)
        held3[c] = jnp.dot(bt_ref[...], d_spec, preferred_element_type=f32).astype(bf16)
        return carry

    lax.fori_loop(0, wide, backward, 0)
    start_all(*fourth)
    keep1 = pltpu.make_async_copy(held3.at[:, rows_of(me), :], back1_ref.at[channels_of(me)], own.at[3])
    keep1.start()
    keep3.wait()
    wait_all(*third)
    keep1.wait()
    wait_all(*fourth)


def exchange(one, three, kern, second_block, third_block, n):
    dma = pltpu.SemaphoreType.DMA
    vmem = pl.BlockSpec(memory_space=pltpu.VMEM)
    hbm = pl.BlockSpec(memory_space=pl.ANY)
    return pl.pallas_call(
        functools.partial(exchange_kernel, n),
        out_shape=(
            jax.ShapeDtypeStruct(one.shape, bf16),
            jax.ShapeDtypeStruct(three.shape, bf16),
            jax.ShapeDtypeStruct(kern.shape, bf16),
        ),
        in_specs=[hbm, hbm] + [vmem] * 5,
        out_specs=(hbm, hbm, vmem),
        scratch_shapes=[
            pltpu.VMEM(kern.shape, bf16),
            pltpu.VMEM(kern.shape, bf16),
            pltpu.VMEM(kern.shape, f32),
        ] + [dma((n,))] * 8 + [dma((4,))],
        compiler_params=pltpu.CompilerParams(collective_id=1, has_side_effects=True),
        name="exchange",
    )(one, three, kern, second_block, second_block.T, third_block, third_block.T)


def on_device(tokens, w_value, w_gate, first_block, second_block, third_block, fourth_block, kernel, skip_gain, cotangent):
    n = lax.axis_size("seq")
    n1 = second_block.shape[0]
    n2 = first_block.shape[0]
    local_rows, d = tokens.shape
    rows_here = n1 // n
    value = jnp.dot(tokens, w_value, preferred_element_type=f32).astype(bf16)
    cube = value.reshape(rows_here, n2, d)
    section_one = jnp.einsum("abc,pb->cap", cube, first_block, preferred_element_type=f32).astype(bf16)
    gate = jnp.dot(tokens, w_gate, preferred_element_type=f32).astype(bf16)
    upstream = cotangent.astype(f32)
    d_mix = (upstream * gate.astype(f32)).astype(bf16)
    d_mix_cube = d_mix.reshape(rows_here, n2, d)
    d_three = jnp.einsum("rsc,sp->crp", d_mix_cube, fourth_block, preferred_element_type=f32).astype(bf16)
    skip_term = jnp.sum(d_mix.astype(f32) * value.astype(f32), axis=0)
    back_three, back_one, grad_kernel = exchange(section_one, d_three, kernel, second_block, third_block, n)
    conv = jnp.einsum("crp,sp->rsc", back_three, fourth_block, preferred_element_type=f32)
    mixed = conv.reshape(local_rows, d) + skip_gain * value.astype(f32)
    d_gate = (upstream * mixed).astype(bf16)
    factor = 1.0 / jnp.sqrt(jnp.asarray(n1 * n2, f32))
    gate_term = (jnp.dot(tokens.T, d_gate, preferred_element_type=f32) * factor).astype(bf16)
    gate_grad = jnp.dot(d_gate, w_gate.T, preferred_element_type=f32)

    d_cube = jnp.einsum("cap,pb->abc", back_one, first_block, preferred_element_type=f32)
    d_value = (d_cube.reshape(local_rows, d) + skip_gain * d_mix.astype(f32)).astype(bf16)
    grad_tokens = (jnp.dot(d_value, w_value.T, preferred_element_type=f32) + gate_grad).astype(bf16)
    value_term = (jnp.dot(tokens.T, d_value, preferred_element_type=f32) * factor).astype(bf16)
    skip_rows = jnp.pad((skip_term * factor).reshape(-1, 128), ((0, 8 - d // 128), (0, 0)))
    sums, skip_sum = all_sum(jnp.concatenate([value_term, gate_term]), skip_rows, n)
    return (grad_tokens, grad_kernel, sums.astype(f32).reshape(2, d, d), skip_sum[: d // 128].reshape(d))


def solution(mesh):
    in_specs = (
        P(("parts", "seq"), None), P(), P(), P(), P(), P(), P(), P("seq", None, None), P(), P(("parts", "seq"), None),
    )
    out_specs = (
        P(("parts", "seq"), None), P(("parts", "seq"), None, None), P("parts", None, None), P("parts"),
    )
    return jax.shard_map(on_device, mesh=mesh, in_specs=in_specs, out_specs=out_specs, check_vma=False)
```

```python
import functools

import jax
import jax.numpy as jnp
from jax import lax
from jax.experimental import pallas as pl
from jax.experimental.pallas import tpu as pltpu
from jax.sharding import PartitionSpec as P

MESH = pl.DeviceIdType.MESH
f32 = jnp.float32
bf16 = jnp.bfloat16


def reduce_kernel(n, x_ref, s_ref, out_ref, skip_ref, pair, mine, slots, skips, rs_send, rs_recv, ag_send, ag_recv, fw_send, fw_recv, sk_send, sk_recv, ps_send, ps_recv):
    me = lax.axis_index("seq")
    core = lax.rem(me, 2)
    chip = lax.div(me, 2)
    chips = n // 2
    partner = me + 1 - 2 * core
    rows = x_ref.shape[0]
    half = rows // 2
    part = half // chips

    barrier = pltpu.get_barrier_semaphore()

    def greet(k, carry):
        peer = lax.rem(me + k, n)
        pl.semaphore_signal(barrier, inc=1, device_id={"seq": peer}, device_id_type=MESH)
        return carry

    lax.fori_loop(1, n, greet, 0)
    pl.semaphore_wait(barrier, n - 1)

    other_half = pl.ds(pl.multiple_of((1 - core) * half, half), half)
    first = pltpu.make_async_remote_copy(
        src_ref=x_ref.at[other_half], dst_ref=pair, send_sem=ps_send, recv_sem=ps_recv,
        device_id={"seq": partner}, device_id_type=MESH)
    first.start()

    def skip_copy(k):
        peer = lax.rem(me + k, n)
        return pltpu.make_async_remote_copy(
            src_ref=s_ref, dst_ref=skips.at[k], send_sem=sk_send.at[k], recv_sem=sk_recv.at[k],
            device_id={"seq": peer}, device_id_type=MESH)

    lax.fori_loop(1, n, lambda k, c: (skip_copy(k).start(), c)[1], 0)
    first.wait()
    my_half = pl.ds(pl.multiple_of(core * half, half), half)
    mine[...] = (x_ref[my_half, :].astype(f32) + pair[...].astype(f32)).astype(bf16)

    def rs_copy(k):
        peer_chip = lax.rem(chip + k, chips)
        src = pl.ds(pl.multiple_of(peer_chip * part, part), part)
        return pltpu.make_async_remote_copy(
            src_ref=mine.at[src], dst_ref=slots.at[k], send_sem=rs_send.at[k], recv_sem=rs_recv.at[k],
            device_id={"seq": 2 * peer_chip + core}, device_id_type=MESH)

    lax.fori_loop(1, chips, lambda k, c: (rs_copy(k).start(), c)[1], 0)
    own = pl.ds(pl.multiple_of(chip * part, part), part)

    def rs_add(k, total):
        rs_copy(k).wait_recv()
        return total + slots[k].astype(f32)

    total = lax.fori_loop(1, chips, rs_add, mine[own, :].astype(f32))
    lax.fori_loop(1, chips, lambda k, c: (rs_copy(k).wait_send(), c)[1], 0)
    place = pl.ds(pl.multiple_of(core * half + chip * part, part), part)
    out_ref[place, :] = total.astype(bf16)

    def rows_of(k):
        source = lax.rem(chip - k + chips, chips)
        return pl.ds(pl.multiple_of(core * half + source * part, part), part)

    def ag_copy(k):
        peer_chip = lax.rem(chip + k, chips)
        return pltpu.make_async_remote_copy(
            src_ref=out_ref.at[place], dst_ref=out_ref.at[place], send_sem=ag_send.at[k], recv_sem=ag_recv.at[k],
            device_id={"seq": 2 * peer_chip + core}, device_id_type=MESH)

    def pass_on(k):
        return pltpu.make_async_remote_copy(
            src_ref=out_ref.at[rows_of(k)], dst_ref=out_ref.at[rows_of(k)], send_sem=fw_send.at[k], recv_sem=fw_recv.at[k],
            device_id={"seq": partner}, device_id_type=MESH)

    lax.fori_loop(1, chips, lambda k, c: (ag_copy(k).start(), c)[1], 0)
    pass_on(0).start()

    skips[0] = s_ref[...]
    lax.fori_loop(1, n, lambda k, c: (skip_copy(k).wait(), c)[1], 0)

    def skip_add(d, total):
        return total + skips[lax.rem(me - d + n, n)]

    skip_ref[...] = lax.fori_loop(0, n, skip_add, jnp.zeros(s_ref.shape, f32))

    def arrived(k, carry):
        ag_copy(k).wait_recv()
        pass_on(k).start()
        return carry

    lax.fori_loop(1, chips, arrived, 0)
    lax.fori_loop(1, chips, lambda k, c: (ag_copy(k).wait_send(), c)[1], 0)
    lax.fori_loop(0, chips, lambda k, c: (pass_on(k).wait(), c)[1], 0)


def all_sum(x, s, n):
    rows, cols = x.shape
    half = rows // 2
    chips = n // 2
    dma = pltpu.SemaphoreType.DMA
    return pl.pallas_call(
        functools.partial(reduce_kernel, n),
        out_shape=(jax.ShapeDtypeStruct(x.shape, bf16), jax.ShapeDtypeStruct(s.shape, f32)),
        in_specs=[pl.BlockSpec(memory_space=pltpu.VMEM)] * 2,
        out_specs=(pl.BlockSpec(memory_space=pltpu.VMEM),) * 2,
        scratch_shapes=[
            pltpu.VMEM((half, cols), bf16),
            pltpu.VMEM((half, cols), bf16),
            pltpu.VMEM((chips, half // chips, cols), bf16),
            pltpu.VMEM((n,) + s.shape, f32),
            dma((chips,)), dma((chips,)), dma((chips,)), dma((chips,)), dma((chips,)), dma((chips,)), dma((n,)), dma((n,)), dma, dma,
        ],
        compiler_params=pltpu.CompilerParams(collective_id=0, has_side_effects=True),
        name="all_sum",
    )(x, s)


def flip(x):
    return x.astype(f32).T.astype(bf16)


def dot(x, y, left, right):
    return lax.dot_general(x, y, (((left,), (right,)), ((), ())), preferred_element_type=f32)


def mixer_kernel(n, factor, tok_ref, cot_ref, kern_hbm, wv_ref, wg_ref, f_ref, b_ref, g_ref, h_ref, gain_ref,
                 gtok_hbm, gk_hbm, back3_hbm, back1_hbm, terms_ref, skip_ref,
                 value, d_mix, kern, one, three, held1, held3, work, spec, acc, ft, bt, gt,
                 s1, r1, s3, r3, sb3, rb3, sb1, rb1, own, rows_sem):
    me = lax.axis_index("seq")
    wide = kern.shape[0]
    total_rows = held1.shape[0]
    rows = tok_ref.shape[0]
    dim = tok_ref.shape[2]
    load = pltpu.make_async_copy(kern_hbm, kern, own.at[4])
    load.start()
    barrier = pltpu.get_barrier_semaphore()

    def greet(k, carry):
        pl.semaphore_signal(barrier, inc=1, device_id={"seq": lax.rem(me + k, n)}, device_id_type=MESH)
        return carry

    lax.fori_loop(1, n, greet, 0)

    ft[...] = flip(f_ref[...])
    bt[...] = flip(b_ref[...])
    gt[...] = flip(g_ref[...])

    def section_one(a, carry):
        v = jnp.dot(tok_ref[a], wv_ref[...], preferred_element_type=f32).astype(bf16)
        value[a] = v
        one[a] = dot(v, ft[...], 0, 0).astype(bf16)
        return carry

    lax.fori_loop(0, rows, section_one, 0)
    pl.semaphore_wait(barrier, n - 1)

    def channels_of(d):
        return pl.ds(pl.multiple_of(d * wide, wide), wide)

    def rows_of(d):
        return pl.ds(d * rows, rows)

    def out_copy(src, dst, send, recv, k):
        peer = lax.rem(me + k, n)
        return pltpu.make_async_remote_copy(
            src_ref=src.at[:, channels_of(peer), :], dst_ref=dst.at[rows_of(me)], send_sem=send.at[k], recv_sem=recv.at[k],
            device_id={"seq": peer}, device_id_type=MESH)

    def back_copy(src, dst, send, recv, k):
        peer = lax.rem(me + k, n)
        return pltpu.make_async_remote_copy(
            src_ref=src.at[rows_of(peer)], dst_ref=dst.at[:, channels_of(me), :], send_sem=send.at[k], recv_sem=recv.at[k],
            device_id={"seq": peer}, device_id_type=MESH)

    def start_all(copy, *refs):
        def go(i, carry):
            k = n // 2 + (2 * lax.rem(i, 2) - 1) * lax.div(i + 1, 2)
            copy(*refs, k).start()
            return carry

        lax.fori_loop(0, n - 1, go, 0)

    def wait_all(copy, *refs):
        lax.fori_loop(1, n, lambda k, c: (copy(*refs, k).wait(), c)[1], 0)

    first = (out_copy, one, held1, s1, r1)
    second = (out_copy, three, held3, s3, r3)
    third = (back_copy, held1, back3_hbm, sb3, rb3)
    fourth = (back_copy, held3, back1_hbm, sb1, rb1)
    start_all(*first)
    own1 = pltpu.make_async_copy(one.at[:, channels_of(me), :], held1.at[rows_of(me)], own.at[0])
    own1.start()

    def section_three_back(a, total):
        up = cot_ref[a].astype(f32)
        gate = jnp.dot(tok_ref[a], wg_ref[...], preferred_element_type=f32).astype(bf16)
        m = (up * gate.astype(f32)).astype(bf16)
        d_mix[a] = m
        three[a] = dot(m, h_ref[...], 0, 0).astype(bf16)
        return total + jnp.sum(m.astype(f32) * value[a].astype(f32), axis=0, keepdims=True)

    skip_ref[...] = lax.fori_loop(0, rows, section_three_back, jnp.zeros((1, dim), f32)) * factor
    own3 = pltpu.make_async_copy(three.at[:, channels_of(me), :], held3.at[rows_of(me)], own.at[1])
    own3.start()
    start_all(*second)

    def gather(src):
        def step(i, carry):
            at = pl.ds(pl.multiple_of(i * 16, 16), 16)
            work[:, at, :] = jnp.swapaxes(src[at], 0, 1)
            return carry

        lax.fori_loop(0, total_rows // 16, step, 0)

    def scatter(dst):
        def step(i, carry):
            at = pl.ds(pl.multiple_of(i * 16, 16), 16)
            dst[at] = jnp.swapaxes(work[:, at, :], 0, 1)
            return carry

        lax.fori_loop(0, total_rows // 16, step, 0)

    own1.wait()
    load.wait()
    wait_all(*first)
    gather(held1)

    def forward(c, carry):
        spectrum = jnp.dot(b_ref[...], work[c], preferred_element_type=f32)
        spec[c] = spectrum
        filtered = (spectrum * kern[c].astype(f32)).astype(bf16)
        work[c] = jnp.dot(g_ref[...], filtered, preferred_element_type=f32).astype(bf16)
        return carry

    lax.fori_loop(0, wide, forward, 0)
    scatter(held1)
    start_all(*third)
    keep3 = pltpu.make_async_copy(held1.at[rows_of(me)], back3_hbm.at[:, channels_of(me), :], own.at[2])
    keep3.start()
    own3.wait()
    wait_all(*second)
    gather(held3)

    def backward(c, carry):
        d_freq = jnp.dot(gt[...], work[c], preferred_element_type=f32)
        d_spec = (d_freq * kern[c].astype(f32)).astype(bf16)
        kern[c] = (d_freq * spec[c]).astype(bf16)
        work[c] = jnp.dot(bt[...], d_spec, preferred_element_type=f32).astype(bf16)
        return carry

    lax.fori_loop(0, wide, backward, 0)
    scatter(held3)
    start_all(*fourth)
    keep1 = pltpu.make_async_copy(held3.at[rows_of(me)], back1_hbm.at[:, channels_of(me), :], own.at[3])
    keep1.start()
    store = pltpu.make_async_copy(kern, gk_hbm, own.at[5])
    store.start()

    keep3.wait()
    wait_all(*third)
    fetch3 = pltpu.make_async_copy(back3_hbm, one, own.at[6])
    fetch3.start()
    fetch3.wait()
    acc[...] = jnp.zeros_like(acc)

    def gate_part(r, carry):
        conv = dot(h_ref[...], one[r], 1, 1)
        mixed = conv + gain_ref[...] * value[r].astype(f32)
        d_gate = (cot_ref[r].astype(f32) * mixed).astype(bf16)
        value[r] = d_gate
        acc[...] += dot(tok_ref[r], d_gate, 0, 0)
        return carry

    lax.fori_loop(0, rows, gate_part, 0)
    terms_ref[pl.ds(dim, dim), :] = (acc[...] * factor).astype(bf16)
    acc[...] = jnp.zeros_like(acc)

    store.wait()
    keep1.wait()
    wait_all(*fourth)
    fetch1 = pltpu.make_async_copy(back1_hbm, three, own.at[7])
    fetch1.start()
    fetch1.wait()

    def row_copy(r):
        return pltpu.make_async_copy(d_mix.at[r], gtok_hbm.at[r], rows_sem.at[r])

    def value_part(r, carry):
        cube = dot(ft[...], three[r], 1, 1)
        d_value = (cube + gain_ref[...] * d_mix[r].astype(f32)).astype(bf16)
        acc[...] += dot(tok_ref[r], d_value, 0, 0)
        d_mix[r] = (dot(d_value, wv_ref[...], 1, 1) + dot(value[r], wg_ref[...], 1, 1)).astype(bf16)
        row_copy(r).start()
        return carry

    lax.fori_loop(0, rows, value_part, 0)
    terms_ref[pl.ds(0, dim), :] = (acc[...] * factor).astype(bf16)
    lax.fori_loop(0, rows, lambda r, c: (row_copy(r).wait(), c)[1], 0)


def on_device(tokens, w_value, w_gate, first_block, second_block, third_block, fourth_block, kernel, skip_gain, cotangent):
    n = lax.axis_size("seq")
    n1 = second_block.shape[0]
    n2 = first_block.shape[0]
    local_rows, d = tokens.shape
    rows = n1 // n
    wide = kernel.shape[0]
    factor = float(n1 * n2) ** -0.5
    dma = pltpu.SemaphoreType.DMA
    vmem = pl.BlockSpec(memory_space=pltpu.VMEM)
    hbm = pl.BlockSpec(memory_space=pl.ANY)
    by_row = (rows, n2, d)
    on_link = (rows, d, n2)
    square = pltpu.VMEM((n1, n1), bf16)
    grad_tokens, grad_kernel, _, _, terms, skip_term = pl.pallas_call(
        functools.partial(mixer_kernel, n, factor),
        out_shape=(
            jax.ShapeDtypeStruct(by_row, bf16),
            jax.ShapeDtypeStruct(kernel.shape, bf16),
            jax.ShapeDtypeStruct(on_link, bf16),
            jax.ShapeDtypeStruct(on_link, bf16),
            jax.ShapeDtypeStruct((2 * d, d), bf16),
            jax.ShapeDtypeStruct((1, d), f32),
        ),
        in_specs=[vmem, vmem, hbm] + [vmem] * 7,
        out_specs=(hbm, hbm, hbm, hbm, vmem, vmem),
        scratch_shapes=[
            pltpu.VMEM(by_row, bf16),
            pltpu.VMEM(by_row, bf16),
            pltpu.VMEM(kernel.shape, bf16),
            pltpu.VMEM(on_link, bf16),
            pltpu.VMEM(on_link, bf16),
            pltpu.VMEM((n1, wide, n2), bf16),
            pltpu.VMEM((n1, wide, n2), bf16),
            pltpu.VMEM((wide, n1, n2), bf16),
            pltpu.VMEM((wide, n1, n2), f32),
            pltpu.VMEM((d, d), f32),
            pltpu.VMEM((n2, n2), bf16), square, square,
        ] + [dma((n,))] * 8 + [dma((8,)), dma((rows,))],
        compiler_params=pltpu.CompilerParams(collective_id=1, has_side_effects=True, vmem_limit_bytes=66_000_000),
        name="mixer",
    )(tokens.reshape(by_row), cotangent.reshape(by_row), kernel, w_value, w_gate, first_block, second_block,
      third_block, fourth_block, skip_gain.reshape(1, d))
    skip_rows = jnp.pad(skip_term.reshape(-1, 128), ((0, 8 - d // 128), (0, 0)))
    sums, skip_sum = all_sum(terms, skip_rows, n)
    return (grad_tokens.reshape(local_rows, d), grad_kernel, sums.astype(f32).reshape(2, d, d), skip_sum[: d // 128].reshape(d))


def solution(mesh):
    in_specs = (
        P(("parts", "seq"), None), P(), P(), P(), P(), P(), P(), P("seq", None, None), P(), P(("parts", "seq"), None),
    )
    out_specs = (
        P(("parts", "seq"), None), P(("parts", "seq"), None, None), P("parts", None, None), P("parts"),
    )
    return jax.shard_map(on_device, mesh=mesh, in_specs=in_specs, out_specs=out_specs, check_vma=False)
```

```python
import functools

import jax
import jax.numpy as jnp
from jax import lax
from jax.experimental import pallas as pl
from jax.experimental.pallas import tpu as pltpu
from jax.sharding import PartitionSpec as P

MESH = pl.DeviceIdType.MESH
PIECES = 4
f32 = jnp.float32
bf16 = jnp.bfloat16


def reduce_kernel(n, x_ref, s_ref, out_ref, skip_ref, pair, mine, slots, skips, rs_send, rs_recv, ag_send, ag_recv, fw_send, fw_recv, sk_send, sk_recv, ps_send, ps_recv):
    me = lax.axis_index("seq")
    core = lax.rem(me, 2)
    chip = lax.div(me, 2)
    chips = n // 2
    partner = me + 1 - 2 * core
    rows = x_ref.shape[0]
    half = rows // 2
    part = half // chips

    barrier = pltpu.get_barrier_semaphore()

    def greet(k, carry):
        peer = lax.rem(me + k, n)
        pl.semaphore_signal(barrier, inc=1, device_id={"seq": peer}, device_id_type=MESH)
        return carry

    lax.fori_loop(1, n, greet, 0)
    pl.semaphore_wait(barrier, n - 1)

    other_half = pl.ds(pl.multiple_of((1 - core) * half, half), half)
    first = pltpu.make_async_remote_copy(
        src_ref=x_ref.at[other_half], dst_ref=pair, send_sem=ps_send, recv_sem=ps_recv,
        device_id={"seq": partner}, device_id_type=MESH)
    first.start()

    def skip_copy(k):
        peer = lax.rem(me + k, n)
        return pltpu.make_async_remote_copy(
            src_ref=s_ref, dst_ref=skips.at[k], send_sem=sk_send.at[k], recv_sem=sk_recv.at[k],
            device_id={"seq": peer}, device_id_type=MESH)

    lax.fori_loop(1, n, lambda k, c: (skip_copy(k).start(), c)[1], 0)
    first.wait()
    my_half = pl.ds(pl.multiple_of(core * half, half), half)
    mine[...] = (x_ref[my_half, :].astype(f32) + pair[...].astype(f32)).astype(bf16)

    def rs_copy(k):
        peer_chip = lax.rem(chip + k, chips)
        src = pl.ds(pl.multiple_of(peer_chip * part, part), part)
        return pltpu.make_async_remote_copy(
            src_ref=mine.at[src], dst_ref=slots.at[k], send_sem=rs_send.at[k], recv_sem=rs_recv.at[k],
            device_id={"seq": 2 * peer_chip + core}, device_id_type=MESH)

    lax.fori_loop(1, chips, lambda k, c: (rs_copy(k).start(), c)[1], 0)
    own = pl.ds(pl.multiple_of(chip * part, part), part)

    def rs_add(k, total):
        rs_copy(k).wait_recv()
        return total + slots[k].astype(f32)

    total = lax.fori_loop(1, chips, rs_add, mine[own, :].astype(f32))
    lax.fori_loop(1, chips, lambda k, c: (rs_copy(k).wait_send(), c)[1], 0)
    place = pl.ds(pl.multiple_of(core * half + chip * part, part), part)
    out_ref[place, :] = total.astype(bf16)

    def rows_of(k):
        source = lax.rem(chip - k + chips, chips)
        return pl.ds(pl.multiple_of(core * half + source * part, part), part)

    def ag_copy(k):
        peer_chip = lax.rem(chip + k, chips)
        return pltpu.make_async_remote_copy(
            src_ref=out_ref.at[place], dst_ref=out_ref.at[place], send_sem=ag_send.at[k], recv_sem=ag_recv.at[k],
            device_id={"seq": 2 * peer_chip + core}, device_id_type=MESH)

    def pass_on(k):
        return pltpu.make_async_remote_copy(
            src_ref=out_ref.at[rows_of(k)], dst_ref=out_ref.at[rows_of(k)], send_sem=fw_send.at[k], recv_sem=fw_recv.at[k],
            device_id={"seq": partner}, device_id_type=MESH)

    lax.fori_loop(1, chips, lambda k, c: (ag_copy(k).start(), c)[1], 0)
    pass_on(0).start()

    skips[0] = s_ref[...]
    lax.fori_loop(1, n, lambda k, c: (skip_copy(k).wait(), c)[1], 0)

    def skip_add(d, total):
        return total + skips[lax.rem(me - d + n, n)]

    skip_ref[...] = lax.fori_loop(0, n, skip_add, jnp.zeros(s_ref.shape, f32))

    def arrived(k, carry):
        ag_copy(k).wait_recv()
        pass_on(k).start()
        return carry

    lax.fori_loop(1, chips, arrived, 0)
    lax.fori_loop(1, chips, lambda k, c: (ag_copy(k).wait_send(), c)[1], 0)
    lax.fori_loop(0, chips, lambda k, c: (pass_on(k).wait(), c)[1], 0)


def all_sum(x, s, n):
    rows, cols = x.shape
    half = rows // 2
    chips = n // 2
    dma = pltpu.SemaphoreType.DMA
    return pl.pallas_call(
        functools.partial(reduce_kernel, n),
        out_shape=(jax.ShapeDtypeStruct(x.shape, bf16), jax.ShapeDtypeStruct(s.shape, f32)),
        in_specs=[pl.BlockSpec(memory_space=pltpu.VMEM)] * 2,
        out_specs=(pl.BlockSpec(memory_space=pltpu.VMEM),) * 2,
        scratch_shapes=[
            pltpu.VMEM((half, cols), bf16),
            pltpu.VMEM((half, cols), bf16),
            pltpu.VMEM((chips, half // chips, cols), bf16),
            pltpu.VMEM((n,) + s.shape, f32),
            dma((chips,)), dma((chips,)), dma((chips,)), dma((chips,)), dma((chips,)), dma((chips,)), dma((n,)), dma((n,)), dma, dma,
        ],
        compiler_params=pltpu.CompilerParams(collective_id=0, has_side_effects=True),
        name="all_sum",
    )(x, s)


def flip(x):
    return x.astype(f32).T.astype(bf16)


def dot(x, y, left, right):
    return lax.dot_general(x, y, (((left,), (right,)), ((), ())), preferred_element_type=f32)


def mixer_kernel(n, factor, tok_ref, cot_ref, kern_hbm, wv_ref, wg_ref, f_ref, b_ref, g_ref, h_ref, gain_ref,
                 gtok_hbm, gk_hbm, back3_hbm, back1_hbm, terms_ref, skip_ref,
                 value, d_mix, kern, one, three, held1, held3, work, spec, acc, ft, bt, gt,
                 s1, r1, s3, r3, sb3, rb3, sb1, rb1, own, rows_sem):
    me = lax.axis_index("seq")
    wide = kern.shape[0]
    total_rows = held1.shape[0]
    rows = tok_ref.shape[0]
    dim = tok_ref.shape[2]
    load = pltpu.make_async_copy(kern_hbm, kern, own.at[4])
    load.start()
    barrier = pltpu.get_barrier_semaphore()

    def greet(k, carry):
        pl.semaphore_signal(barrier, inc=1, device_id={"seq": lax.rem(me + k, n)}, device_id_type=MESH)
        return carry

    lax.fori_loop(1, n, greet, 0)

    ft[...] = flip(f_ref[...])
    bt[...] = flip(b_ref[...])
    gt[...] = flip(g_ref[...])

    def channels_of(d):
        return pl.ds(pl.multiple_of(d * wide, wide), wide)

    def rows_of(d):
        return pl.ds(d * rows, rows)

    def out_copy(src, dst, send, recv, k):
        peer = lax.rem(me + k, n)
        return pltpu.make_async_remote_copy(
            src_ref=src.at[:, channels_of(peer), :], dst_ref=dst.at[rows_of(me)], send_sem=send.at[k], recv_sem=recv.at[k],
            device_id={"seq": peer}, device_id_type=MESH)

    def back_copy(src, dst, send, recv, k):
        peer = lax.rem(me + k, n)
        return pltpu.make_async_remote_copy(
            src_ref=src.at[rows_of(peer)], dst_ref=dst.at[:, channels_of(me), :], send_sem=send.at[k], recv_sem=recv.at[k],
            device_id={"seq": peer}, device_id_type=MESH)

    def start_all(copy, *refs):
        def go(i, carry):
            k = n // 2 + (2 * lax.rem(i, 2) - 1) * lax.div(i + 1, 2)
            copy(*refs, k).start()
            return carry

        lax.fori_loop(0, n - 1, go, 0)

    def wait_all(copy, *refs):
        lax.fori_loop(1, n, lambda k, c: (copy(*refs, k).wait(), c)[1], 0)

    slab = rows // PIECES

    def first_piece(h):
        def copy(k):
            peer = lax.rem(me + k, n)
            return pltpu.make_async_remote_copy(
                src_ref=one.at[pl.ds(h * slab, slab), channels_of(peer), :],
                dst_ref=held1.at[pl.ds(me * rows + h * slab, slab)],
                send_sem=s1.at[h * n + k], recv_sem=r1.at[h * n + k],
                device_id={"seq": peer}, device_id_type=MESH)

        return copy

    def fourth_piece(h):
        def copy(k):
            peer = lax.rem(me + k, n)
            return pltpu.make_async_remote_copy(
                src_ref=held3.at[pl.ds(peer * rows + h * slab, slab)],
                dst_ref=back1_hbm.at[pl.ds(h * slab, slab), channels_of(me), :],
                send_sem=sb1.at[h * n + k], recv_sem=rb1.at[h * n + k],
                device_id={"seq": peer}, device_id_type=MESH)

        return copy

    second = (out_copy, three, held3, s3, r3)
    third = (back_copy, held1, back3_hbm, sb3, rb3)
    def section_one(a, carry):
        v = jnp.dot(tok_ref[a], wv_ref[...], preferred_element_type=f32).astype(bf16)
        value[a] = v
        one[a] = dot(v, ft[...], 0, 0).astype(bf16)
        return carry

    pl.semaphore_wait(barrier, n - 1)
    for h in range(PIECES):
        lax.fori_loop(h * slab, (h + 1) * slab, section_one, 0)
        start_all(first_piece(h))
    own1 = pltpu.make_async_copy(one.at[:, channels_of(me), :], held1.at[rows_of(me)], own.at[0])
    own1.start()

    def section_three_back(a, total):
        up = cot_ref[a].astype(f32)
        gate = jnp.dot(tok_ref[a], wg_ref[...], preferred_element_type=f32).astype(bf16)
        m = (up * gate.astype(f32)).astype(bf16)
        d_mix[a] = m
        three[a] = dot(m, h_ref[...], 0, 0).astype(bf16)
        return total + jnp.sum(m.astype(f32) * value[a].astype(f32), axis=0, keepdims=True)

    skip_ref[...] = lax.fori_loop(0, rows, section_three_back, jnp.zeros((1, dim), f32)) * factor
    own3 = pltpu.make_async_copy(three.at[:, channels_of(me), :], held3.at[rows_of(me)], own.at[1])
    own3.start()
    start_all(*second)

    def gather(src):
        def step(i, carry):
            at = pl.ds(pl.multiple_of(i * 16, 16), 16)
            work[:, at, :] = jnp.swapaxes(src[at], 0, 1)
            return carry

        lax.fori_loop(0, total_rows // 16, step, 0)

    def scatter(dst):
        def step(i, carry):
            at = pl.ds(pl.multiple_of(i * 16, 16), 16)
            dst[at] = jnp.swapaxes(work[:, at, :], 0, 1)
            return carry

        lax.fori_loop(0, total_rows // 16, step, 0)

    own1.wait()
    load.wait()
    for h in range(PIECES):
        wait_all(first_piece(h))
    gather(held1)

    def forward(c, carry):
        spectrum = jnp.dot(b_ref[...], work[c], preferred_element_type=f32)
        spec[c] = spectrum
        filtered = (spectrum * kern[c].astype(f32)).astype(bf16)
        work[c] = jnp.dot(g_ref[...], filtered, preferred_element_type=f32).astype(bf16)
        return carry

    lax.fori_loop(0, wide, forward, 0)
    scatter(held1)
    start_all(*third)
    keep3 = pltpu.make_async_copy(held1.at[rows_of(me)], back3_hbm.at[:, channels_of(me), :], own.at[2])
    keep3.start()
    own3.wait()
    wait_all(*second)
    gather(held3)

    def backward(c, carry):
        d_freq = jnp.dot(gt[...], work[c], preferred_element_type=f32)
        d_spec = (d_freq * kern[c].astype(f32)).astype(bf16)
        kern[c] = (d_freq * spec[c]).astype(bf16)
        work[c] = jnp.dot(bt[...], d_spec, preferred_element_type=f32).astype(bf16)
        return carry

    lax.fori_loop(0, wide, backward, 0)
    scatter(held3)
    for h in range(PIECES):
        start_all(fourth_piece(h))
    keep1 = pltpu.make_async_copy(held3.at[rows_of(me)], back1_hbm.at[:, channels_of(me), :], own.at[3])
    keep1.start()
    store = pltpu.make_async_copy(kern, gk_hbm, own.at[5])
    store.start()

    keep3.wait()
    wait_all(*third)
    fetch3 = pltpu.make_async_copy(back3_hbm, one, own.at[6])
    fetch3.start()
    fetch3.wait()
    acc[...] = jnp.zeros_like(acc)

    def gate_part(r, carry):
        conv = dot(h_ref[...], one[r], 1, 1)
        mixed = conv + gain_ref[...] * value[r].astype(f32)
        d_gate = (cot_ref[r].astype(f32) * mixed).astype(bf16)
        value[r] = d_gate
        acc[...] += dot(tok_ref[r], d_gate, 0, 0)
        return carry

    lax.fori_loop(0, rows, gate_part, 0)
    terms_ref[pl.ds(dim, dim), :] = (acc[...] * factor).astype(bf16)
    acc[...] = jnp.zeros_like(acc)

    store.wait()
    keep1.wait()

    def row_copy(r):
        return pltpu.make_async_copy(d_mix.at[r], gtok_hbm.at[r], rows_sem.at[r])

    def value_part(r, carry):
        cube = dot(ft[...], three[r], 1, 1)
        d_value = (cube + gain_ref[...] * d_mix[r].astype(f32)).astype(bf16)
        acc[...] += dot(tok_ref[r], d_value, 0, 0)
        d_mix[r] = (dot(d_value, wv_ref[...], 1, 1) + dot(value[r], wg_ref[...], 1, 1)).astype(bf16)
        row_copy(r).start()
        return carry

    for h in range(PIECES):
        wait_all(fourth_piece(h))
        at = pl.ds(h * slab, slab)
        fetch1 = pltpu.make_async_copy(back1_hbm.at[at], three.at[at], own.at[7])
        fetch1.start()
        fetch1.wait()
        lax.fori_loop(h * slab, (h + 1) * slab, value_part, 0)
    terms_ref[pl.ds(0, dim), :] = (acc[...] * factor).astype(bf16)
    lax.fori_loop(0, rows, lambda r, c: (row_copy(r).wait(), c)[1], 0)


def on_device(tokens, w_value, w_gate, first_block, second_block, third_block, fourth_block, kernel, skip_gain, cotangent):
    n = lax.axis_size("seq")
    n1 = second_block.shape[0]
    n2 = first_block.shape[0]
    local_rows, d = tokens.shape
    rows = n1 // n
    wide = kernel.shape[0]
    factor = float(n1 * n2) ** -0.5
    dma = pltpu.SemaphoreType.DMA
    vmem = pl.BlockSpec(memory_space=pltpu.VMEM)
    hbm = pl.BlockSpec(memory_space=pl.ANY)
    by_row = (rows, n2, d)
    on_link = (rows, d, n2)
    square = pltpu.VMEM((n1, n1), bf16)
    grad_tokens, grad_kernel, _, _, terms, skip_term = pl.pallas_call(
        functools.partial(mixer_kernel, n, factor),
        out_shape=(
            jax.ShapeDtypeStruct(by_row, bf16),
            jax.ShapeDtypeStruct(kernel.shape, bf16),
            jax.ShapeDtypeStruct(on_link, bf16),
            jax.ShapeDtypeStruct(on_link, bf16),
            jax.ShapeDtypeStruct((2 * d, d), bf16),
            jax.ShapeDtypeStruct((1, d), f32),
        ),
        in_specs=[vmem, vmem, hbm] + [vmem] * 7,
        out_specs=(hbm, hbm, hbm, hbm, vmem, vmem),
        scratch_shapes=[
            pltpu.VMEM(by_row, bf16),
            pltpu.VMEM(by_row, bf16),
            pltpu.VMEM(kernel.shape, bf16),
            pltpu.VMEM(on_link, bf16),
            pltpu.VMEM(on_link, bf16),
            pltpu.VMEM((n1, wide, n2), bf16),
            pltpu.VMEM((n1, wide, n2), bf16),
            pltpu.VMEM((wide, n1, n2), bf16),
            pltpu.VMEM((wide, n1, n2), f32),
            pltpu.VMEM((d, d), f32),
            pltpu.VMEM((n2, n2), bf16), square, square,
        ] + [dma((PIECES * n,))] * 2 + [dma((n,))] * 4 + [dma((PIECES * n,))] * 2 + [dma((8,)), dma((rows,))],
        compiler_params=pltpu.CompilerParams(collective_id=1, has_side_effects=True, vmem_limit_bytes=66_000_000),
        name="mixer",
    )(tokens.reshape(by_row), cotangent.reshape(by_row), kernel, w_value, w_gate, first_block, second_block,
      third_block, fourth_block, skip_gain.reshape(1, d))
    skip_rows = jnp.pad(skip_term.reshape(-1, 128), ((0, 8 - d // 128), (0, 0)))
    sums, skip_sum = all_sum(terms, skip_rows, n)
    return (grad_tokens.reshape(local_rows, d), grad_kernel, sums.astype(f32).reshape(2, d, d), skip_sum[: d // 128].reshape(d))


def solution(mesh):
    in_specs = (
        P(("parts", "seq"), None), P(), P(), P(), P(), P(), P(), P("seq", None, None), P(), P(("parts", "seq"), None),
    )
    out_specs = (
        P(("parts", "seq"), None), P(("parts", "seq"), None, None), P("parts", None, None), P("parts"),
    )
    return jax.shard_map(on_device, mesh=mesh, in_specs=in_specs, out_specs=out_specs, check_vma=False)
```
